32 devices in a mesh: gx: 8 (over z, x), gy: 4 (over y, core).
Axes of the slice: x: 2, y: 2, z: 4, core: 2. Of those that a mesh axis runs over, the one named last changes fastest.
Arguments:
- right_side: float32 [8, 32, 64, 512], P(None, 'gx', 'gy'), may hold values from -6 to 6
- velocity: float32 [3, 32, 64, 512], P(None, 'gx', 'gy'), may hold values from -0.5 to 0.5
- reaction: float32 [32, 64, 512], P('gx', 'gy'), may hold values from 0.1 to 2
Outputs:
- solution: float32 [8, 32, 64, 512], P(None, 'gx', 'gy')
- residual: float32 [8, 32, 64, 512], P(None, 'gx', 'gy')
The draws below stay inside these ranges and needn't reach their ends.
All inputs are finite; a program needn't handle non-finite values.
Results may differ from the reference program's by a relative error of at most 0.00045.
Values sent between devices are 32-bit elements; how exact they have to be, the bound alone decides.
No kernel may reach another device: no remote copies, remote signals or barrier semaphores. Data moves between devices by JAX's collectives and lax.ppermute only.
A program may use at most 64 MiB of HBM per device.

```python
import math
import jax
import jax.numpy as jnp
import numpy as np
from jax import lax

CZ = 512
NRHS = 8
S = 4
ITERS = 2
NX = 32
NY = 64


def block_scale(rng, dims, split, smallest, high):
    def one(axis_at, blocks):
        heights = jax.random.uniform(jax.random.fold_in(jax.random.fold_in(rng, 6), axis_at), (blocks,), jnp.float32, smallest / len(split), high / len(split))
        return jnp.repeat(jnp.exp(heights), dims[axis_at] // blocks).reshape((-1,) + (1,) * (len(dims) - axis_at - 1))

    factor_of = one(*split[0])
    for cut in split[1:]:
        factor_of = factor_of * one(*cut)
    return factor_of


def noise(rng, shape, width, bound, shards=(), kind=jnp.bfloat16):
    result = width * jax.random.normal(rng, shape, jnp.float32)
    if shards:
        result = result * block_scale(rng, shape, shards, -0.22, 0.18)
    return jnp.clip(result, -bound, bound).astype(kind)


def setup_inputs(seed: int = 0) -> dict:
    key_list = jax.random.split(jax.random.key(seed), 4)
    right_side = noise(key_list[0], (NRHS, NX, NY, CZ), 1.0, 6.0, ((1, 8), (2, 4)), jnp.float32)
    velocity = jnp.clip(jax.random.uniform(key_list[1], (3, NX, NY, CZ), jnp.float32, -0.5, 0.5) * block_scale(key_list[1], (3, NX, NY, CZ), ((1, 8), (2, 4)), -0.4, 0.0), -0.5, 0.5)
    reaction = jnp.clip(jnp.exp(math.log(2.0) - 2.9957323 * jax.random.uniform(key_list[2], (NX, NY, CZ), jnp.float32) ** block_scale(key_list[2], (NX, NY, CZ), ((0, 8), (1, 4)), -0.2, 0.2)), 0.1, 2.0)
    return dict(right_side=right_side, velocity=velocity, reaction=reaction)


def apply_padded(padded, velocity, reaction):
    center = padded[:, 1:-1, 1:-1, 1:-1]
    neighbours = (1.0 - velocity[0]) * padded[:, 2:, 1:-1, 1:-1]
    neighbours = neighbours + (1.0 + velocity[0]) * padded[:, :-2, 1:-1, 1:-1]
    neighbours = neighbours + (1.0 - velocity[1]) * padded[:, 1:-1, 2:, 1:-1]
    neighbours = neighbours + (1.0 + velocity[1]) * padded[:, 1:-1, :-2, 1:-1]
    neighbours = neighbours + (1.0 - velocity[2]) * padded[:, 1:-1, 1:-1, 2:]
    neighbours = neighbours + (1.0 + velocity[2]) * padded[:, 1:-1, 1:-1, :-2]
    return (6.0 + reaction) * center - neighbours

def krylov_tables(nrhs, degree):
    total = (degree + 1) * nrhs
    mixing = np.zeros((total, degree * nrhs), np.float32)
    for column in range(degree * nrhs):
        mixing[column, column] = 6.0
        mixing[column + nrhs, column] = 6.0
    starting = np.zeros((total, nrhs), np.float32)
    starting[:nrhs] = np.eye(nrhs, dtype=np.float32)
    lifting = np.zeros((total, degree * nrhs), np.float32)
    lifting[:degree * nrhs] = np.eye(degree * nrhs, dtype=np.float32)
    return (jnp.asarray(mixing, jnp.float32), jnp.asarray(starting, jnp.float32), jnp.asarray(lifting, jnp.float32))

def solve_step(gram, nrhs, degree):
    mixing, starting, lifting = krylov_tables(nrhs, degree)
    highest = lax.Precision.HIGHEST
    mixed = jnp.dot(mixing.T, gram, precision=highest)
    normal = jnp.dot(mixed, mixing, precision=highest)
    target = jnp.dot(mixed, starting, precision=highest)
    factor = jnp.linalg.cholesky(normal)
    middle = lax.linalg.triangular_solve(factor, target, left_side=True, lower=True)
    update = lax.linalg.triangular_solve(factor, middle, left_side=True, lower=True, transpose_a=True)
    residual_coef = starting - jnp.dot(mixing, update, precision=highest)
    solution_coef = jnp.dot(lifting, update, precision=highest)
    return jnp.concatenate([solution_coef, residual_coef], axis=1)

def reference(right_side, velocity, reaction):
    nrhs = right_side.shape[0]
    highest = lax.Precision.HIGHEST
    solution = jnp.zeros_like(right_side)
    residual = right_side
    for outer_step in range(ITERS):
        basis = [residual]
        for power_step in range(S):
            current = basis[-1]
            padded = jnp.pad(current, ((0, 0), (1, 1), (1, 1), (1, 1)))
            image = apply_padded(padded, velocity, reaction)
            basis.append((image - 6.0 * current) / 6.0)
        stacked = jnp.stack(basis).reshape((S + 1) * nrhs, -1)
        gram = lax.dot_general(stacked, stacked, (((1,), (1,)), ((), ())), precision=highest)
        coefs = solve_step(gram, nrhs, S)
        combined = lax.dot_general(coefs, stacked, (((0,), (0,)), ((), ())), precision=highest)
        solution = solution + combined[:nrhs].reshape(right_side.shape)
        residual = combined[nrhs:].reshape(right_side.shape)
    return (solution, residual)
```

```python
import functools
import jax
import jax.numpy as jnp
import numpy as np
from jax import lax
from jax.experimental import pallas as pl
from jax.experimental.pallas import tpu as pltpu
from jax.sharding import PartitionSpec as P

S = 4
ITERS = 2
W = 2
AXES = ("gx", "gy")


def shifted(cells, dx, dy):
    nx, ny = lax.axis_size("gx"), lax.axis_size("gy")
    if dy == 0:
        return lax.ppermute(cells, "gx", [(i, i + dx) for i in range(nx) if 0 <= i + dx < nx])
    if dx == 0:
        return lax.ppermute(cells, "gy", [(i, i + dy) for i in range(ny) if 0 <= i + dy < ny])
    pairs = [
        (i * ny + j, (i + dx) * ny + j + dy)
        for i in range(nx)
        for j in range(ny)
        if 0 <= i + dx < nx and 0 <= j + dy < ny
    ]
    return lax.ppermute(cells, AXES, pairs)


def halo(field):
    lx, ly = field.shape[:2]
    return (
        shifted(field[lx - W :], 1, 0),
        shifted(field[:W], -1, 0),
        shifted(field[:, ly - W :], 0, 1),
        shifted(field[:, :W], 0, -1),
        shifted(field[lx - 1 :, ly - 1 :], 1, 1),
        shifted(field[lx - 1 :, :1], 1, -1),
        shifted(field[:1, ly - 1 :], -1, 1),
        shifted(field[:1, :1], -1, -1),
    )


def coefficients(velocity, reaction):
    lx, ly, cz = reaction.shape
    fields = jnp.concatenate([velocity, reaction[None]], axis=0)
    xlo = shifted(fields[:, lx - 1 :], 1, 0)
    xhi = shifted(fields[:, :1], -1, 0)
    ylo = shifted(fields[:, :, ly - 1 :], 0, 1)
    yhi = shifted(fields[:, :, :1], 0, -1)
    side = ((0, 0), (0, 0), (1, 1), (0, 0))
    middle = jnp.concatenate([ylo, fields, yhi], axis=2)
    full = jnp.concatenate([jnp.pad(xlo, side), middle, jnp.pad(xhi, side)], axis=1)
    ix = lax.axis_index("gx") * lx + jnp.arange(lx + 2) - 1
    iy = lax.axis_index("gy") * ly + jnp.arange(ly + 2) - 1
    inx = (ix >= 0) & (ix < lx * lax.axis_size("gx"))
    iny = (iy >= 0) & (iy < ly * lax.axis_size("gy"))
    inside = (inx[:, None] & iny[None, :])[:, :, None]
    iz = jnp.arange(cz)
    v, r = full[:3], full[3]
    sixth = 1.0 / 6.0
    parts = [
        r * sixth,
        (v[0] - 1.0) * sixth,
        (-1.0 - v[0]) * sixth,
        (v[1] - 1.0) * sixth,
        (-1.0 - v[1]) * sixth,
        jnp.where(iz < cz - 1, (v[2] - 1.0) * sixth, 0.0),
        jnp.where(iz > 0, (-1.0 - v[2]) * sixth, 0.0),
    ]
    return jnp.stack([jnp.where(inside, part, 0.0) for part in parts])


def powers_kernel(p, xlo, xhi, ylo, yhi, cll, clh, chl, chh, coef, out1, out2, ext, mid):
    lx, ly, nrhs, cz = p.shape
    for i in range(lx):
        ext[i + W, W : W + ly] = p[i]
        ext[i + W, 0:W] = ylo[i]
        ext[i + W, W + ly : W + ly + W] = yhi[i]
    for i in range(W):
        ext[i, W : W + ly] = xlo[i]
        ext[lx + W + i, W : W + ly] = xhi[i]
    ext[1, 1] = cll[0, 0]
    ext[1, W + ly] = clh[0, 0]
    ext[lx + W, 1] = chl[0, 0]
    ext[lx + W, W + ly] = chh[0, 0]

    def row(src, x, y, cx, cy):
        def c(k):
            return jnp.broadcast_to(coef[k, cx, cy : cy + 1, :], (nrhs, cz))

        here = src[x, y]
        acc = c(0) * here
        acc = acc + c(1) * src[x + 1, y]
        acc = acc + c(2) * src[x - 1, y]
        acc = acc + c(3) * src[x, y + 1]
        acc = acc + c(4) * src[x, y - 1]
        acc = acc + c(5) * pltpu.roll(here, cz - 1, 1)
        acc = acc + c(6) * pltpu.roll(here, 1, 1)
        return acc

    def first(x, _):
        for y in range(1, ly + 1):
            mid[x, y] = row(ext, x + 1, y + 1, x, y)
        return 0

    lax.fori_loop(0, lx + 2, first, 0)

    def first_sides(x, _):
        for y in (0, ly + 1):
            mid[x, y] = row(ext, x + 1, y + 1, x, y)
        return 0

    lax.fori_loop(1, lx + 1, first_sides, 0)

    def second(x, _):
        for y in range(ly):
            out1[x, y] = mid[x + 1, y + 1]
            out2[x, y] = row(mid, x + 1, y + 1, x + 1, y + 1)
        return 0

    lax.fori_loop(0, lx, second, 0)


def two_powers(field, coef):
    lx, ly, nrhs, cz = field.shape
    like = jax.ShapeDtypeStruct(field.shape, jnp.float32)
    return pl.pallas_call(
        powers_kernel,
        out_shape=(like, like),
        scratch_shapes=[
            pltpu.VMEM((lx + 2 * W, ly + 2 * W, nrhs, cz), jnp.float32),
            pltpu.VMEM((lx + 2, ly + 2, nrhs, cz), jnp.float32),
        ],
        name="powers",
    )(field, *halo(field), coef)


def gram_kernel(*refs):
    *basis, out = refs
    lx, ly, nrhs, cz = basis[0].shape
    total = nrhs * len(basis)

    def body(x, acc):
        for y in range(ly):
            slab = jnp.concatenate([b[x, y] for b in basis], axis=0)
            hi = slab.astype(jnp.bfloat16)
            lo = (slab - hi.astype(jnp.float32)).astype(jnp.bfloat16)
            both = jnp.concatenate([hi, lo], axis=0)
            acc = acc + lax.dot_general(
                both, both, (((1,), (1,)), ((), ())), preferred_element_type=jnp.float32
            )
        return acc

    acc = lax.fori_loop(0, lx, body, jnp.zeros((2 * total, 2 * total), jnp.float32))
    cross = acc[:total, total:]
    out[...] = acc[:total, :total] + (cross + acc[total:, :total]) + acc[total:, total:]


def local_gram(basis):
    total = basis[0].shape[2] * len(basis)
    return pl.pallas_call(
        gram_kernel, out_shape=jax.ShapeDtypeStruct((total, total), jnp.float32), name="gram"
    )(*basis)


def krylov_tables(nrhs, degree):
    total = (degree + 1) * nrhs
    mixing = np.zeros((total, degree * nrhs), np.float32)
    for column in range(degree * nrhs):
        mixing[column, column] = 6.0
        mixing[column + nrhs, column] = 6.0
    starting = np.zeros((total, nrhs), np.float32)
    starting[:nrhs] = np.eye(nrhs, dtype=np.float32)
    lifting = np.zeros((total, degree * nrhs), np.float32)
    lifting[: degree * nrhs] = np.eye(degree * nrhs, dtype=np.float32)
    return (
        jnp.asarray(mixing, jnp.float32),
        jnp.asarray(starting, jnp.float32),
        jnp.asarray(lifting, jnp.float32),
    )


def solve_step(gram, nrhs, degree):
    mixing, starting, lifting = krylov_tables(nrhs, degree)
    highest = lax.Precision.HIGHEST
    mixed = jnp.dot(mixing.T, gram, precision=highest)
    normal = jnp.dot(mixed, mixing, precision=highest)
    target = jnp.dot(mixed, starting, precision=highest)
    factor = jnp.linalg.cholesky(normal)
    middle = lax.linalg.triangular_solve(factor, target, left_side=True, lower=True)
    update = lax.linalg.triangular_solve(
        factor, middle, left_side=True, lower=True, transpose_a=True
    )
    residual_coef = starting - jnp.dot(mixing, update, precision=highest)
    solution_coef = jnp.dot(lifting, update, precision=highest)
    return jnp.concatenate([solution_coef, residual_coef], axis=1)


def global_gram(gram):
    for axis in ("gy", "gx"):
        count = lax.axis_size(axis)
        step = 1
        while step < count:
            gram = gram + lax.ppermute(gram, axis, [(i, i ^ step) for i in range(count)])
            step *= 2
    return gram


def combine_kernel(*refs):
    *basis, coefs, out = refs
    lx, ly, nrhs, cz = basis[0].shape

    def body(x, _):
        for y in range(ly):
            slab = jnp.concatenate([b[x, y] for b in basis], axis=0)
            out[x, y] = jnp.dot(
                coefs[...],
                slab,
                precision=lax.Precision.HIGHEST,
                preferred_element_type=jnp.float32,
            )
        return 0

    lax.fori_loop(0, lx, body, 0)


def combine(basis, coefs):
    lx, ly, nrhs, cz = basis[0].shape
    return pl.pallas_call(
        combine_kernel,
        out_shape=jax.ShapeDtypeStruct((lx, ly, coefs.shape[1], cz), jnp.float32),
        name="combine",
    )(*basis, coefs.T)


def local(right_side, velocity, reaction):
    nrhs = right_side.shape[0]
    coef = coefficients(velocity, reaction)
    residual = right_side.transpose(1, 2, 0, 3)
    total = None
    for outer_step in range(ITERS):
        basis = [residual]
        for _ in range(S // 2):
            basis.extend(two_powers(basis[-1], coef))
        coefs = solve_step(global_gram(local_gram(basis)), nrhs, S)
        combined = combine(basis, coefs)
        part = combined[:, :, :nrhs]
        total = part if total is None else total + part
        residual = combined[:, :, nrhs:]
    return (total.transpose(2, 0, 1, 3), residual.transpose(2, 0, 1, 3))


def solution(mesh):
    in_specs = (P(None, "gx", "gy", None), P(None, "gx", "gy", None), P("gx", "gy", None))
    out_specs = (P(None, "gx", "gy", None), P(None, "gx", "gy", None))
    return jax.shard_map(local, mesh=mesh, in_specs=in_specs, out_specs=out_specs, check_vma=False)
```

```python
import functools
import jax
import jax.numpy as jnp
import numpy as np
from jax import lax
from jax.experimental import pallas as pl
from jax.experimental.pallas import tpu as pltpu
from jax.sharding import PartitionSpec as P


S = 4
ITERS = 2
W = 2
AXES = ("gx", "gy")


def shifted(cells, dx, dy):
    nx, ny = lax.axis_size("gx"), lax.axis_size("gy")
    if dy == 0:
        return lax.ppermute(cells, "gx", [(i, i + dx) for i in range(nx) if 0 <= i + dx < nx])
    if dx == 0:
        return lax.ppermute(cells, "gy", [(i, i + dy) for i in range(ny) if 0 <= i + dy < ny])
    pairs = [
        (i * ny + j, (i + dx) * ny + j + dy)
        for i in range(nx)
        for j in range(ny)
        if 0 <= i + dx < nx and 0 <= j + dy < ny
    ]
    return lax.ppermute(cells, AXES, pairs)


def edges(field):
    lx, ly = field.shape[:2]
    return field[lx - W :], field[:W], field[:, ly - W :], field[:, :W]


def halo(sends):
    xtail, xhead, ytail, yhead = sends
    xlo = shifted(xtail, 1, 0)
    xhi = shifted(xhead, -1, 0)
    ylo = shifted(ytail, 0, 1)
    yhi = shifted(yhead, 0, -1)
    lx = ylo.shape[0]
    clo = shifted(jnp.stack([ylo[lx - 1, W - 1], yhi[lx - 1, 0]]), 1, 0)
    chi = shifted(jnp.stack([ylo[0, W - 1], yhi[0, 0]]), -1, 0)
    return xlo, xhi, ylo, yhi, clo, chi


def coefficients(velocity, reaction):
    lx, ly, cz = reaction.shape
    fields = jnp.concatenate([velocity, reaction[None]], axis=0)
    xlo = shifted(fields[:, lx - 1 :], 1, 0)
    xhi = shifted(fields[:, :1], -1, 0)
    ylo = shifted(fields[:, :, ly - 1 :], 0, 1)
    yhi = shifted(fields[:, :, :1], 0, -1)
    side = ((0, 0), (0, 0), (1, 1), (0, 0))
    middle = jnp.concatenate([ylo, fields, yhi], axis=2)
    full = jnp.concatenate([jnp.pad(xlo, side), middle, jnp.pad(xhi, side)], axis=1)
    ix = lax.axis_index("gx") * lx + jnp.arange(lx + 2) - 1
    iy = lax.axis_index("gy") * ly + jnp.arange(ly + 2) - 1
    inx = (ix >= 0) & (ix < lx * lax.axis_size("gx"))
    iny = (iy >= 0) & (iy < ly * lax.axis_size("gy"))
    inside = (inx[:, None] & iny[None, :])[:, :, None]
    iz = jnp.arange(cz)
    v, r = full[:3], full[3]
    sixth = 1.0 / 6.0
    parts = [
        r * sixth,
        (v[0] - 1.0) * sixth,
        (-1.0 - v[0]) * sixth,
        (v[1] - 1.0) * sixth,
        (-1.0 - v[1]) * sixth,
        jnp.where(iz < cz - 1, (v[2] - 1.0) * sixth, 0.0),
        jnp.where(iz > 0, (-1.0 - v[2]) * sixth, 0.0),
    ]
    return jnp.stack([jnp.where(inside, part, 0.0) for part in parts])


def powers_kernel(p, xlo, xhi, ylo, yhi, clo, chi, coef, out1, out2, *rest):
    *sends, ext, mid = rest
    lx, ly, nrhs, cz = p.shape
    for i in range(lx):
        ext[i + W, W : W + ly] = p[i]
        ext[i + W, 0:W] = ylo[i]
        ext[i + W, W + ly : W + ly + W] = yhi[i]
    for i in range(W):
        ext[i, W : W + ly] = xlo[i]
        ext[lx + W + i, W : W + ly] = xhi[i]
    ext[1, 1] = clo[0]
    ext[1, W + ly] = clo[1]
    ext[lx + W, 1] = chi[0]
    ext[lx + W, W + ly] = chi[1]

    def row(src, x, y, cx, cy):
        def c(k):
            return jnp.broadcast_to(coef[k, cx, cy : cy + 1, :], (nrhs, cz))

        here = src[x, y]
        acc = c(0) * here
        acc = acc + c(1) * src[x + 1, y]
        acc = acc + c(2) * src[x - 1, y]
        acc = acc + c(3) * src[x, y + 1]
        acc = acc + c(4) * src[x, y - 1]
        acc = acc + c(5) * pltpu.roll(here, cz - 1, 1)
        acc = acc + c(6) * pltpu.roll(here, 1, 1)
        return acc

    def first(x, _):
        for y in range(1, ly + 1):
            mid[x, y] = row(ext, x + 1, y + 1, x, y)
        return 0

    lax.fori_loop(0, lx + 2, first, 0)

    def first_sides(x, _):
        for y in (0, ly + 1):
            mid[x, y] = row(ext, x + 1, y + 1, x, y)
        return 0

    lax.fori_loop(1, lx + 1, first_sides, 0)

    def second(x, _):
        for y in range(ly):
            out1[x, y] = mid[x + 1, y + 1]
            out2[x, y] = row(mid, x + 1, y + 1, x + 1, y + 1)
        return 0

    lax.fori_loop(0, lx, second, 0)
    if sends:
        xtail, xhead, ytail, yhead = sends
        xtail[...] = out2[lx - W :]
        xhead[...] = out2[:W]
        ytail[...] = out2[:, ly - W :]
        yhead[...] = out2[:, :W]


def two_powers(field, received, coef, emit):
    lx, ly, nrhs, cz = field.shape
    shapes = [field.shape, field.shape]
    if emit:
        shapes += [(W, ly, nrhs, cz)] * 2 + [(lx, W, nrhs, cz)] * 2
    return pl.pallas_call(
        powers_kernel,
        out_shape=[jax.ShapeDtypeStruct(shape, jnp.float32) for shape in shapes],
        scratch_shapes=[
            pltpu.VMEM((lx + 2 * W, ly + 2 * W, nrhs, cz), jnp.float32),
            pltpu.VMEM((lx + 2, ly + 2, nrhs, cz), jnp.float32),
        ],
        name="powers",
    )(field, *received, coef)


def gram_kernel(*refs):
    *basis, out = refs
    lx, ly, nrhs, cz = basis[0].shape
    total = nrhs * len(basis)

    def body(x, acc):
        for y in range(ly):
            slab = jnp.concatenate([b[x, y] for b in basis], axis=0)
            hi = slab.astype(jnp.bfloat16)
            lo = (slab - hi.astype(jnp.float32)).astype(jnp.bfloat16)
            both = jnp.concatenate([hi, lo], axis=0)
            acc = acc + lax.dot_general(
                both, both, (((1,), (1,)), ((), ())), preferred_element_type=jnp.float32
            )
        return acc

    acc = lax.fori_loop(0, lx, body, jnp.zeros((2 * total, 2 * total), jnp.float32))
    cross = acc[:total, total:]
    out[...] = acc[:total, :total] + (cross + acc[total:, :total]) + acc[total:, total:]


def local_gram(basis):
    total = basis[0].shape[2] * len(basis)
    return pl.pallas_call(
        gram_kernel, out_shape=jax.ShapeDtypeStruct((total, total), jnp.float32), name="gram"
    )(*basis)


def krylov_tables(nrhs, degree):
    total = (degree + 1) * nrhs
    mixing = np.zeros((total, degree * nrhs), np.float32)
    for column in range(degree * nrhs):
        mixing[column, column] = 6.0
        mixing[column + nrhs, column] = 6.0
    starting = np.zeros((total, nrhs), np.float32)
    starting[:nrhs] = np.eye(nrhs, dtype=np.float32)
    lifting = np.zeros((total, degree * nrhs), np.float32)
    lifting[: degree * nrhs] = np.eye(degree * nrhs, dtype=np.float32)
    return (
        jnp.asarray(mixing, jnp.float32),
        jnp.asarray(starting, jnp.float32),
        jnp.asarray(lifting, jnp.float32),
    )


def solve_step(gram, nrhs, degree):
    mixing, starting, lifting = krylov_tables(nrhs, degree)
    highest = lax.Precision.HIGHEST
    mixed = jnp.dot(mixing.T, gram, precision=highest)
    normal = jnp.dot(mixed, mixing, precision=highest)
    target = jnp.dot(mixed, starting, precision=highest)
    factor = jnp.linalg.cholesky(normal)
    middle = lax.linalg.triangular_solve(factor, target, left_side=True, lower=True)
    update = lax.linalg.triangular_solve(
        factor, middle, left_side=True, lower=True, transpose_a=True
    )
    residual_coef = starting - jnp.dot(mixing, update, precision=highest)
    solution_coef = jnp.dot(lifting, update, precision=highest)
    return jnp.concatenate([solution_coef, residual_coef], axis=1)


def global_gram(gram):
    for axis in ("gy", "gx"):
        count = lax.axis_size(axis)
        step = 1
        while step < count:
            gram = gram + lax.ppermute(gram, axis, [(i, i ^ step) for i in range(count)])
            step *= 2
    return gram


def combine_kernel(*refs):
    *basis, coefs, out = refs
    lx, ly, nrhs, cz = basis[0].shape

    def body(x, _):
        for y in range(ly):
            slab = jnp.concatenate([b[x, y] for b in basis], axis=0)
            out[x, y] = jnp.dot(
                coefs[...],
                slab,
                precision=lax.Precision.HIGHEST,
                preferred_element_type=jnp.float32,
            )
        return 0

    lax.fori_loop(0, lx, body, 0)


def combine(basis, coefs):
    lx, ly, nrhs, cz = basis[0].shape
    return pl.pallas_call(
        combine_kernel,
        out_shape=jax.ShapeDtypeStruct((lx, ly, coefs.shape[1], cz), jnp.float32),
        name="combine",
    )(*basis, coefs.T)


def local(right_side, velocity, reaction):
    nrhs = right_side.shape[0]
    coef = coefficients(velocity, reaction)
    residual = right_side.transpose(1, 2, 0, 3)
    total = None
    for outer_step in range(ITERS):
        basis = [residual]
        sends = edges(residual)
        for part in range(S // W):
            one, two, *sends = two_powers(basis[-1], halo(sends), coef, part + 1 < S // W)
            basis += [one, two]
        coefs = solve_step(global_gram(local_gram(basis)), nrhs, S)
        combined = combine(basis, coefs)
        part = combined[:, :, :nrhs]
        total = part if total is None else total + part
        residual = combined[:, :, nrhs:]
    return (total.transpose(2, 0, 1, 3), residual.transpose(2, 0, 1, 3))


def solution(mesh):
    in_specs = (P(None, "gx", "gy", None), P(None, "gx", "gy", None), P("gx", "gy", None))
    out_specs = (P(None, "gx", "gy", None), P(None, "gx", "gy", None))
    return jax.shard_map(local, mesh=mesh, in_specs=in_specs, out_specs=out_specs, check_vma=False)
```

```python
import functools
import jax
import jax.numpy as jnp
import numpy as np
from jax import lax
from jax.experimental import pallas as pl
from jax.experimental.pallas import tpu as pltpu
from jax.sharding import PartitionSpec as P


S = 4
ITERS = 2
W = 2
AXES = ("gx", "gy")


def shifted(cells, dx, dy):
    nx, ny = lax.axis_size("gx"), lax.axis_size("gy")
    if dy == 0:
        return lax.ppermute(cells, "gx", [(i, i + dx) for i in range(nx) if 0 <= i + dx < nx])
    if dx == 0:
        return lax.ppermute(cells, "gy", [(i, i + dy) for i in range(ny) if 0 <= i + dy < ny])
    pairs = [
        (i * ny + j, (i + dx) * ny + j + dy)
        for i in range(nx)
        for j in range(ny)
        if 0 <= i + dx < nx and 0 <= j + dy < ny
    ]
    return lax.ppermute(cells, AXES, pairs)


def edges(field):
    lx, ly = field.shape[:2]
    return field[lx - W :], field[:W], field[:, ly - W :], field[:, :W]


def halo(sends, beside=None):
    xtail, xhead, ytail, yhead = sends
    xlo = shifted(xtail, 1, 0)
    xhi = shifted(xhead, -1, 0)
    ylo = shifted(ytail, 0, 1)
    yhi = shifted(yhead, 0, -1)
    lx = ylo.shape[0]
    clo_send = jnp.stack([ylo[lx - 1, W - 1], yhi[lx - 1, 0]])
    chi_send = jnp.stack([ylo[0, W - 1], yhi[0, 0]])
    clo = shifted(clo_send, 1, 0)
    chi = shifted(chi_send, -1, 0)
    if beside is None:
        return (xlo, xhi, ylo, yhi, clo, chi), None
    result = beside(clo_send)
    xlo, xhi, clo, chi, result = lax.optimization_barrier((xlo, xhi, clo, chi, result))
    return (xlo, xhi, ylo, yhi, clo, chi), result


def coefficients(velocity, reaction):
    lx, ly, cz = reaction.shape
    fields = jnp.concatenate([velocity, reaction[None]], axis=0)
    xlo = shifted(fields[:, lx - 1 :], 1, 0)
    xhi = shifted(fields[:, :1], -1, 0)
    ylo = shifted(fields[:, :, ly - 1 :], 0, 1)
    yhi = shifted(fields[:, :, :1], 0, -1)
    side = ((0, 0), (0, 0), (1, 1), (0, 0))
    middle = jnp.concatenate([ylo, fields, yhi], axis=2)
    full = jnp.concatenate([jnp.pad(xlo, side), middle, jnp.pad(xhi, side)], axis=1)
    ix = lax.axis_index("gx") * lx + jnp.arange(lx + 2) - 1
    iy = lax.axis_index("gy") * ly + jnp.arange(ly + 2) - 1
    inx = (ix >= 0) & (ix < lx * lax.axis_size("gx"))
    iny = (iy >= 0) & (iy < ly * lax.axis_size("gy"))
    inside = (inx[:, None] & iny[None, :])[:, :, None]
    iz = jnp.arange(cz)
    v, r = full[:3], full[3]
    sixth = 1.0 / 6.0
    parts = [
        r * sixth,
        (v[0] - 1.0) * sixth,
        (-1.0 - v[0]) * sixth,
        (v[1] - 1.0) * sixth,
        (-1.0 - v[1]) * sixth,
        jnp.where(iz < cz - 1, (v[2] - 1.0) * sixth, 0.0),
        jnp.where(iz > 0, (-1.0 - v[2]) * sixth, 0.0),
    ]
    return jnp.stack([jnp.where(inside, part, 0.0) for part in parts])


def powers_kernel(p, xlo, xhi, ylo, yhi, clo, chi, coef, out1, out2, *rest):
    *sends, ext, mid = rest
    lx, ly, nrhs, cz = p.shape
    for i in range(lx):
        ext[i + W, W : W + ly] = p[i]
        ext[i + W, 0:W] = ylo[i]
        ext[i + W, W + ly : W + ly + W] = yhi[i]
    for i in range(W):
        ext[i, W : W + ly] = xlo[i]
        ext[lx + W + i, W : W + ly] = xhi[i]
    ext[1, 1] = clo[0]
    ext[1, W + ly] = clo[1]
    ext[lx + W, 1] = chi[0]
    ext[lx + W, W + ly] = chi[1]

    def row(src, x, y, cx, cy):
        def c(k):
            return jnp.broadcast_to(coef[k, cx, cy : cy + 1, :], (nrhs, cz))

        here = src[x, y]
        acc = c(0) * here
        acc = acc + c(1) * src[x + 1, y]
        acc = acc + c(2) * src[x - 1, y]
        acc = acc + c(3) * src[x, y + 1]
        acc = acc + c(4) * src[x, y - 1]
        acc = acc + c(5) * pltpu.roll(here, cz - 1, 1)
        acc = acc + c(6) * pltpu.roll(here, 1, 1)
        return acc

    def first(x, _):
        for y in range(1, ly + 1):
            mid[x, y] = row(ext, x + 1, y + 1, x, y)
        return 0

    lax.fori_loop(0, lx + 2, first, 0)

    def first_sides(x, _):
        for y in (0, ly + 1):
            mid[x, y] = row(ext, x + 1, y + 1, x, y)
        return 0

    lax.fori_loop(1, lx + 1, first_sides, 0)

    def second(x, _):
        for y in range(ly):
            out1[x, y] = mid[x + 1, y + 1]
            out2[x, y] = row(mid, x + 1, y + 1, x + 1, y + 1)
        return 0

    lax.fori_loop(0, lx, second, 0)
    if sends:
        xtail, xhead, ytail, yhead = sends
        xtail[...] = out2[lx - W :]
        xhead[...] = out2[:W]
        ytail[...] = out2[:, ly - W :]
        yhead[...] = out2[:, :W]


def two_powers(field, received, coef, emit):
    lx, ly, nrhs, cz = field.shape
    shapes = [field.shape, field.shape]
    if emit:
        shapes += [(W, ly, nrhs, cz)] * 2 + [(lx, W, nrhs, cz)] * 2
    return pl.pallas_call(
        powers_kernel,
        out_shape=[jax.ShapeDtypeStruct(shape, jnp.float32) for shape in shapes],
        scratch_shapes=[
            pltpu.VMEM((lx + 2 * W, ly + 2 * W, nrhs, cz), jnp.float32),
            pltpu.VMEM((lx + 2, ly + 2, nrhs, cz), jnp.float32),
        ],
        name="powers",
    )(field, *received, coef)


def add_gram(acc, slab):
    hi = slab.astype(jnp.bfloat16)
    lo = (slab - hi.astype(jnp.float32)).astype(jnp.bfloat16)
    both = jnp.concatenate([hi, lo], axis=0)
    return acc + lax.dot_general(
        both, both, (((1,), (1,)), ((), ())), preferred_element_type=jnp.float32
    )


def finish_gram(acc, out):
    total = out.shape[0]

    @pl.when(pl.program_id(0) == pl.num_programs(0) - 1)
    def _():
        value = acc[...]
        cross = value[:total, total:] + value[total:, :total]
        out[...] = value[:total, :total] + cross + value[total:, total:]


def gram_kernel(*refs):
    *basis, out, acc = refs

    @pl.when(pl.program_id(0) == 0)
    def _():
        acc[...] = jnp.zeros_like(acc)

    value = acc[...]
    for y in range(basis[0].shape[1]):
        value = add_gram(value, jnp.concatenate([b[0, y] for b in basis], axis=0))
    acc[...] = value
    finish_gram(acc, out)


def layers(array):
    return pl.BlockSpec((1,) + array.shape[1:], lambda i: (i, 0, 0, 0))


def whole(shape):
    return pl.BlockSpec(shape, lambda i: (0,) * len(shape))


def local_gram(basis):
    total = basis[0].shape[2] * len(basis)
    return pl.pallas_call(
        gram_kernel,
        grid=(basis[0].shape[0],),
        in_specs=[layers(b) for b in basis],
        out_specs=whole((total, total)),
        out_shape=jax.ShapeDtypeStruct((total, total), jnp.float32),
        scratch_shapes=[pltpu.VMEM((2 * total, 2 * total), jnp.float32)],
        name="gram",
    )(*basis)


def exact_dot(a, b):
    return jnp.dot(a, b, precision=lax.Precision.HIGHEST, preferred_element_type=jnp.float32)


def rebase_kernel(*refs):
    *basis, coefs, out, gram, acc = refs

    @pl.when(pl.program_id(0) == 0)
    def _():
        acc[...] = jnp.zeros_like(acc)

    value = acc[...]
    for y in range(basis[0].shape[1]):
        slab = exact_dot(coefs[...], jnp.concatenate([b[0, y] for b in basis], axis=0))
        out[0, y] = slab
        value = add_gram(value, slab)
    acc[...] = value
    finish_gram(acc, gram)


def rebase(basis, coefs):
    lx, ly, nrhs, cz = basis[0].shape
    total = coefs.shape[0]
    return pl.pallas_call(
        rebase_kernel,
        grid=(lx,),
        in_specs=[layers(b) for b in basis] + [whole(coefs.shape)],
        out_specs=[pl.BlockSpec((1, ly, total, cz), lambda i: (i, 0, 0, 0)), whole((total, total))],
        out_shape=[
            jax.ShapeDtypeStruct((lx, ly, total, cz), jnp.float32),
            jax.ShapeDtypeStruct((total, total), jnp.float32),
        ],
        scratch_shapes=[pltpu.VMEM((2 * total, 2 * total), jnp.float32)],
        name="rebase",
    )(*basis, coefs)


def combine_kernel(*refs):
    *basis, coefs, out1, out2 = refs
    nrhs = out1.shape[0]
    for y in range(basis[0].shape[1]):
        both = exact_dot(coefs[...], jnp.concatenate([b[0, y] for b in basis], axis=0))
        out1[:, 0, y, :] = both[:nrhs]
        out2[:, 0, y, :] = both[nrhs:]


def combine(basis, coefs):
    lx, ly, nrhs, cz = basis[0].shape
    like = jax.ShapeDtypeStruct((nrhs, lx, ly, cz), jnp.float32)
    spec = pl.BlockSpec((nrhs, 1, ly, cz), lambda i: (0, i, 0, 0))
    return pl.pallas_call(
        combine_kernel,
        grid=(lx,),
        in_specs=[layers(b) for b in basis] + [whole(coefs.shape)],
        out_specs=[spec, spec],
        out_shape=[like, like],
        name="combine",
    )(*basis, coefs)


def krylov_tables(nrhs, degree):
    total = (degree + 1) * nrhs
    mixing = np.zeros((total, degree * nrhs), np.float32)
    for column in range(degree * nrhs):
        mixing[column, column] = 6.0
        mixing[column + nrhs, column] = 6.0
    starting = np.zeros((total, nrhs), np.float32)
    starting[:nrhs] = np.eye(nrhs, dtype=np.float32)
    lifting = np.zeros((total, degree * nrhs), np.float32)
    lifting[: degree * nrhs] = np.eye(degree * nrhs, dtype=np.float32)
    return (
        jnp.asarray(mixing, jnp.float32),
        jnp.asarray(starting, jnp.float32),
        jnp.asarray(lifting, jnp.float32),
    )


def solve_step(gram, nrhs, degree):
    mixing, starting, lifting = krylov_tables(nrhs, degree)
    highest = lax.Precision.HIGHEST
    mixed = jnp.dot(mixing.T, gram, precision=highest)
    normal = jnp.dot(mixed, mixing, precision=highest)
    target = jnp.dot(mixed, starting, precision=highest)
    factor = jnp.linalg.cholesky(normal)
    middle = lax.linalg.triangular_solve(factor, target, left_side=True, lower=True)
    update = lax.linalg.triangular_solve(
        factor, middle, left_side=True, lower=True, transpose_a=True
    )
    residual_coef = starting - jnp.dot(mixing, update, precision=highest)
    solution_coef = jnp.dot(lifting, update, precision=highest)
    return jnp.concatenate([solution_coef, residual_coef], axis=1)


def all_rounds():
    rounds = []
    for axis in ("gy", "gx"):
        step = 1
        while step < lax.axis_size(axis):
            rounds.append((axis, step))
            step *= 2
    return rounds


def add_rounds(gram, rounds):
    for axis, step in rounds:
        count = lax.axis_size(axis)
        gram = gram + lax.ppermute(gram, axis, [(i, i ^ step) for i in range(count)])
    return gram


def global_gram(gram):
    return add_rounds(gram, all_rounds())


def local(right_side, velocity, reaction):
    nrhs = right_side.shape[0]
    coef = coefficients(velocity, reaction)
    first = right_side.transpose(1, 2, 0, 3)
    powers = [first]
    sends = edges(first)
    parts = ITERS * S // W
    rounds = all_rounds()
    early = (len(rounds) + 1) // 2
    partial = step1 = None

    def reduce_first(token):
        basis, _ = lax.optimization_barrier((powers[: S + 1], token))
        return add_rounds(local_gram(basis), rounds[:early])

    def solve_first(token):
        gram, _ = lax.optimization_barrier((partial, token))
        return solve_step(add_rounds(gram, rounds[early:]), nrhs, S)

    for part in range(parts):
        if part == S // W:
            received, partial = halo(sends, reduce_first)
        elif part == S // W + 1:
            received, step1 = halo(sends, solve_first)
        else:
            received, _ = halo(sends)
        one, two, *sends = two_powers(powers[-1], received, coef, part + 1 < parts)
        powers += [one, two]
    total = (S + 1) * nrhs
    after = step1[:, nrhs:].T
    shift = jnp.concatenate(
        [jnp.pad(after, ((0, 0), (k * nrhs, (S - k) * nrhs))) for k in range(S + 1)], axis=0
    )
    second, gram = rebase(powers, shift)
    step2 = solve_step(global_gram(gram), nrhs, S)
    before = jnp.concatenate([step1[:, :nrhs].T, jnp.zeros((nrhs, total), jnp.float32)], axis=0)
    coefs = jnp.concatenate([before, step2.T], axis=1)
    return tuple(combine(powers[: S + 1] + [second], coefs))


def solution(mesh):
    in_specs = (P(None, "gx", "gy", None), P(None, "gx", "gy", None), P("gx", "gy", None))
    out_specs = (P(None, "gx", "gy", None), P(None, "gx", "gy", None))
    return jax.shard_map(local, mesh=mesh, in_specs=in_specs, out_specs=out_specs, check_vma=False)
```
